32 devices in a mesh: member: 8 (over z, x), band: 4 (over y, core).
Axes of the slice: x: 2, y: 2, z: 4, core: 2. Of those that a mesh axis runs over, the one named last changes fastest.
Arguments:
- prior: bfloat16 [8, 2, 768, 1536], P('member', None, 'band'), may hold values from -9 to 9
- analysis: bfloat16 [8, 2, 768, 1536], P('member', None, 'band'), may hold values from -6 to 6
- increment: float32 [2, 768, 1536], P(None, 'band'), may hold values from -6 to 6
- truncation: int32 [2], replicated, may hold values from 128 to 511
Outputs:
- members: bfloat16 [8, 2, 768, 1536], P('member', None, 'band')
The draws below stay inside these ranges and needn't reach their ends.
All inputs are finite; a program needn't handle non-finite values.
Results may differ from the reference program's by a relative error of at most 0.001.
Values sent between devices are 32-bit elements; how exact they have to be, the bound alone decides.
No kernel may reach another device: no remote copies, remote signals or barrier semaphores. Data moves between devices by JAX's collectives and lax.ppermute only.
A program may use at most 128 MiB of HBM per device.

```python
import math
import jax
import jax.numpy as jnp
from jax import lax

NLAT = 768
NLON = 1536
MW = 512
LEV = 2
MEMBERS = 8


def block_levels(own_key, dims, split, least, top_value):
    level = 1.0
    for dim, shards_of in split:
        heights = jax.random.uniform(jax.random.fold_in(jax.random.fold_in(own_key, 6), dim), (shards_of,), jnp.float32, least / len(split), top_value / len(split))
        level = level * jnp.repeat(jnp.exp(heights), dims[dim] // shards_of).reshape((-1,) + (1,) * (len(dims) - 1 - dim))
    return level


def noise(stream_key, extent, scale, limit, split=(), kind=jnp.bfloat16):
    factor_of = block_levels(stream_key, extent, split, -0.22, 0.18) if split else 1.0
    entries = jax.random.normal(stream_key, extent, jnp.float32) * scale * factor_of
    return jnp.minimum(jnp.maximum(entries, -limit), limit).astype(kind)


def setup_inputs(seed: int = 0) -> dict:
    splits = jax.random.split(jax.random.key(seed), 5)
    return {
        "prior": noise(splits[0], (MEMBERS, LEV, NLAT, NLON), 1.5, 9.0, ((0, 8), (2, 4))),
        "analysis": noise(splits[1], (MEMBERS, LEV, NLAT, NLON), 1.0, 6.0, ((0, 8), (2, 4))),
        "increment": noise(splits[2], (LEV, NLAT, NLON), 1.0, 6.0, ((1, 4),), jnp.float32),
        "truncation": jax.random.randint(splits[3], (LEV,), MW // 4, MW).astype(jnp.int32),
    }


RELAX = 0.85
SPREAD_FLOOR = 0.25

def zonal_table(nlon, waves):
    column = jnp.arange(nlon, dtype=jnp.int32)[:, None]
    number = jnp.arange(waves, dtype=jnp.int32)[None, :]
    phase = (column * number % nlon).astype(jnp.float32) * (2.0 * math.pi / nlon)
    return jnp.stack([jnp.cos(phase), jnp.sin(phase)], axis=2).reshape(nlon, 2 * waves)

def cosine_table(nlat):
    order = jnp.arange(nlat, dtype=jnp.int32)[:, None]
    place = jnp.arange(nlat, dtype=jnp.int32)[None, :]
    phase = ((2 * place + 1) * order % (4 * nlat)).astype(jnp.float32) * (math.pi / (2.0 * nlat))
    scale = jnp.where(order == 0, jnp.float32(math.sqrt(1.0 / nlat)), jnp.float32(math.sqrt(2.0 / nlat)))
    return scale * jnp.cos(phase)

def column_weights(waves, nlon):
    number = jnp.arange(2 * waves, dtype=jnp.int32) // 2
    return jnp.where(number == 0, jnp.float32(1.0 / nlon), jnp.float32(2.0 / nlon))

def inflation(sums, count):
    mean_b = sums[0] / count
    mean_a = sums[2] / count
    spread_b = jnp.sqrt(jnp.maximum((sums[1] - count * mean_b * mean_b) / (count - 1), 0.0))
    spread_a = jnp.maximum(jnp.sqrt(jnp.maximum((sums[3] - count * mean_a * mean_a) / (count - 1), 0.0)), SPREAD_FLOOR)
    factor = 1.0 + RELAX * (spread_b - spread_a) / spread_a
    return (factor, mean_b - factor * mean_a)

def reference(prior, analysis, increment, truncation):
    count = prior.shape[0]
    b_vals = prior.astype(jnp.float32)
    a_vals = analysis.astype(jnp.float32)
    sums = jnp.stack([lax.optimization_barrier(jnp.sum(b_vals, 0)), lax.optimization_barrier(jnp.sum(b_vals * b_vals, 0)), lax.optimization_barrier(jnp.sum(a_vals, 0)), lax.optimization_barrier(jnp.sum(a_vals * a_vals, 0))])
    factor, shift = inflation(sums, count)
    levels, nlat, nlon = increment.shape
    table = zonal_table(nlon, MW)
    coef = jnp.dot(increment.reshape(levels * nlat, nlon), table, precision=lax.Precision.HIGHEST).reshape(levels, nlat, 2 * MW)
    cosines = cosine_table(nlat)
    spec = jnp.einsum('ki,lim->lkm', cosines, coef, precision=lax.Precision.HIGHEST)
    order = jnp.arange(nlat, dtype=jnp.int32)[:, None]
    number = (jnp.arange(2 * MW, dtype=jnp.int32) // 2)[None, :]
    keep = (order * order + number * number)[None] <= (truncation * truncation)[:, None, None]
    kept = jnp.einsum('ki,lkm->lim', cosines, jnp.where(keep, spec, 0.0), precision=lax.Precision.HIGHEST)
    weighted = kept * column_weights(MW, nlon)
    smooth = jnp.dot(weighted.reshape(levels * nlat, 2 * MW), table.T, precision=lax.Precision.HIGHEST).reshape(levels, nlat, nlon)
    return ((shift + smooth)[None] + factor[None] * a_vals).astype(jnp.bfloat16)
```

```python
import math

import jax
import jax.numpy as jnp
from jax import lax
from jax.sharding import PartitionSpec as P

MW = 512


RELAX = 0.85
SPREAD_FLOOR = 0.25


QUAD = 4


def inflation(sums, count):
    mean_b = sums[0] / count
    mean_a = sums[2] / count
    spread_b = jnp.sqrt(jnp.maximum((sums[1] - count * mean_b * mean_b) / (count - 1), 0.0))
    spread_a = jnp.maximum(
        jnp.sqrt(jnp.maximum((sums[3] - count * mean_a * mean_a) / (count - 1), 0.0)), SPREAD_FLOOR
    )
    factor = 1.0 + RELAX * (spread_b - spread_a) / spread_a
    return (factor, mean_b - factor * mean_a)


def turn(steps, period):
    angle = (steps % period).astype(jnp.float32) * (2.0 * math.pi / period)
    return jnp.cos(angle), jnp.sin(angle)


def split_rows(count):
    fine = 8
    while fine * fine < count or count % fine:
        fine += 8
    return count // fine, fine


def wavenumbers(waves, bands):
    column = jnp.arange(2 * waves, dtype=jnp.int32)
    width = waves // bands
    return (column // (2 * width)) * width + column % width, (column // width) % 2


def zonal_table(nlon, waves, bands):
    number, sine = wavenumbers(waves, bands)
    coarse, fine = split_rows(nlon)
    big = fine * jnp.arange(coarse, dtype=jnp.int32)[:, None] * number[None, :]
    small = 4 * jnp.arange(fine, dtype=jnp.int32)[:, None] * number[None, :] - nlon * sine[None, :]
    cos_b, sin_b = turn(big, nlon)
    cos_s, sin_s = turn(small, 4 * nlon)
    table = cos_b[:, None] * cos_s[None] - sin_b[:, None] * sin_s[None]
    return table.reshape(nlon, 2 * waves)


def cosine_table(nlat):
    order = jnp.arange(nlat, dtype=jnp.int32)
    coarse, fine = split_rows(nlat)
    scale = jnp.where(
        order == 0, jnp.float32(math.sqrt(1.0 / nlat)), jnp.float32(math.sqrt(2.0 / nlat))
    )
    big = 2 * fine * jnp.arange(coarse, dtype=jnp.int32)[:, None] * order[None, :]
    small = (2 * jnp.arange(fine, dtype=jnp.int32)[:, None] + 1) * order[None, :]
    cos_b, sin_b = turn(big, 4 * nlat)
    cos_s, sin_s = turn(small, 4 * nlat)
    cos_s, sin_s = cos_s * scale[None], sin_s * scale[None]
    table = cos_b[:, None] * cos_s[None] - sin_b[:, None] * sin_s[None]
    return table.reshape(nlat, nlat)


def dot(x, y, dims):
    return lax.dot_general(
        x, y, (dims, ((), ())), precision=lax.Precision.HIGH, preferred_element_type=jnp.float32
    )


def truncated(increment, truncation, level, row, rows, cuts):
    levels, lat_rows, nlon = increment.shape
    bands = lax.axis_size("band")
    nlat = bands * lat_rows
    width = 2 * MW // bands
    table = zonal_table(nlon, MW, bands)
    field = lax.dynamic_index_in_dim(increment, level, 0, keepdims=False)
    coef = dot(field, table, ((1,), (0,)))
    coef = coef.reshape(lat_rows, bands, width).transpose(1, 0, 2)
    waves = lax.all_to_all(coef, "band", split_axis=0, concat_axis=0, tiled=True)
    cosines = cosine_table(nlat)
    spec = dot(waves.reshape(nlat, width), cosines, ((0,), (0,)))
    order = jnp.arange(nlat, dtype=jnp.int32)[None, :]
    number, _ = wavenumbers(MW, bands)
    number = lax.dynamic_slice(number, (lax.axis_index("band") * width,), (width,))[:, None]
    limit = lax.dynamic_index_in_dim(truncation, level, 0, keepdims=False)
    weight = jnp.where(number == 0, jnp.float32(1.0 / nlon), jnp.float32(2.0 / nlon))
    spec = jnp.where(order * order + number * number <= limit * limit, spec * weight, 0.0)
    picked = lax.dynamic_slice(
        cosines.reshape(bands, lat_rows, nlat), (0, row, 0), (bands, rows, nlat)
    )
    kept = dot(picked.reshape(bands * rows, nlat), spec, ((1,), (1,))).reshape(bands, rows, width)
    mine = lax.all_to_all(kept, "band", split_axis=0, concat_axis=0, tiled=True)
    mine = mine.transpose(1, 0, 2).reshape(rows, bands * width)
    return [
        dot(mine, lax.dynamic_slice(table, (start, 0), (size, 2 * MW)), ((1,), (1,)))
        for start, size in cuts
    ]


def on_device(prior, analysis, increment, truncation):
    members = lax.axis_size("member")
    quads = members // QUAD
    count = prior.shape[0] * members
    me = lax.axis_index("member")
    seat, quad = me % QUAD, me // QUAD
    before, after = prior[0], analysis[0]
    levels, lat_rows, nlon = before.shape
    half = lat_rows // 2
    wide = 0
    near, far = wide // quads, (nlon - wide) // quads

    def swap(x, k):
        return lax.ppermute(x, "member", [(i, i ^ k) for i in range(members)])

    def corner(s):
        return s & 1, (s >> 1) * half

    def block(x, s, start, size):
        level, row = corner(s)
        return lax.dynamic_slice(x, (level, row, start), (1, half, size))[0]

    def pair(s, start, size):
        both = jnp.stack([block(before, s, start, size), block(after, s, start, size)])
        return lax.optimization_barrier(both.astype(jnp.float32))

    def put(out, change, s, start, size):
        level, row = corner(s)
        value = block(after, s, start, size).astype(jnp.float32) + change
        return lax.dynamic_update_slice(out, value.astype(jnp.bfloat16)[None], (level, row, start))

    level, row = corner(seat)
    here = wide + quad * far

    theirs = [pair(seat, here, far)]
    for k in range(members - 1, 0, -1):
        other = me ^ k
        theirs.append(swap(pair(other % QUAD, wide + (other // QUAD) * far, far), k))
    smooth = truncated(increment, truncation, level, row, half, [(here, far)])[0]
    b_vals = [x[0] for x in theirs]
    a_vals = [x[1] for x in theirs]
    sums = [sum(b_vals), sum(b * b for b in b_vals), sum(a_vals), sum(a * a for a in a_vals)]
    factor, shift = inflation(sums, count)
    base, gain = shift + smooth, factor - 1.0
    out = jnp.zeros((levels, lat_rows, nlon), jnp.bfloat16)
    out = put(out, base + gain * a_vals[0], seat, here, far)
    for i, k in enumerate(range(members - 1, 0, -1)):
        other = me ^ k
        change = swap(base + gain * a_vals[1 + i], k)
        out = put(out, change, other % QUAD, wide + (other // QUAD) * far, far)
    return out[None]


def solution(mesh):
    placed = (
        P("member", None, "band", None),
        P("member", None, "band", None),
        P(None, "band", None),
        P(),
    )
    return jax.shard_map(
        on_device,
        mesh=mesh,
        in_specs=placed,
        out_specs=P("member", None, "band", None),
        check_vma=False,
    )
```
